32 devices in a mesh: dp: 4 (over x, core), seq: 8 (over z, y).
Axes of the slice: x: 2, y: 2, z: 4, core: 2. Of those that a mesh axis runs over, the one named last changes fastest.
Arguments:
- hidden: bfloat16 [8192, 1536], P(('dp', 'seq')), may hold values from -6 to 6
- database: bfloat16 [4, 96, 128, 896], P('dp', 'seq'), may hold values from -8 to 8
- block_home: int32 [96], replicated, may hold values from 0 to 95, as said below
- neighbours: int32 [128, 2], P(('dp', 'seq')), may hold values from 0 to 95, as said below
- neighbour_counts: int32 [128], P(('dp', 'seq')), may hold values from 1 to 2
- encoder_gain: float32 [896], replicated, may hold values from 0.25 to 1.75
- encoder_projection: bfloat16 [896, 2688], replicated, may hold values from -2 to 2
- encoder_output: bfloat16 [896, 896], replicated, may hold values from -0.1875 to 0.1875
- cross_gain: float32 [1536], replicated, may hold values from 0.25 to 1.75
- cross_query: bfloat16 [1536, 1536], replicated, may hold values from -2 to 2
- cross_keyvalue: bfloat16 [3072, 896], replicated, may hold values from -2 to 2
- cross_output: bfloat16 [1536, 1536], replicated, may hold values from -0.15625 to 0.15625
- cotangent: bfloat16 [8192, 1536], P(('dp', 'seq')), may hold values from -6 to 6
Outputs:
- output: bfloat16 [8192, 1536], P(('dp', 'seq'))
- keyvalue_grad: float32 [3072, 896], P('seq')
The draws below stay inside these ranges and needn't reach their ends.
Inputs may be any that keep to these rules, and one draw needn't show every extreme that they name: A permutation: block b lies at position block_home[b] of the second dimension of database. `neighbours`: the 8 ids of one device's spans name at most 2 blocks whose positions lie on the same device of seq, and exactly 2 on some device, on every device. Ids may repeat.
All inputs are finite; a program needn't handle non-finite values.
Results may differ from the reference program's by a relative error of at most 0.02.
Values may be sent and summed in bfloat16 or wider, within the bound.
A program may use at most 128 MiB of HBM per device.

```python
import jax
import jax.numpy as jnp
from jax import lax

D = 1536
E = 896
HEAD = 128
K = 2
SPAN = 64
BLOCK = 128
TOK_DEV = 256
SPANS_DEV = 4
CAP = 2
DB_DEV = 12
DB_BLOCKS = 96
TOKENS = 8192
SPANS = 128
N_DP = 4
N_SEQ = 8


def plan_blocks(key):
    block_home = jax.random.permutation(jax.random.fold_in(key, 11), DB_BLOCKS).astype(jnp.int32)
    inverse = jnp.argsort(block_home).astype(jnp.int32)
    readers = N_DP * N_SEQ
    requests = K * SPANS_DEV
    popular = jax.random.randint(jax.random.fold_in(key, 12), (N_SEQ,), 0, 4)
    noise = jax.random.randint(jax.random.fold_in(key, 13), (readers, N_SEQ), 0, 4 * N_SEQ)
    ranking = (noise + 3 * N_SEQ * popular[None, :]) * N_SEQ + jnp.arange(N_SEQ)[None, :]
    ranked = jnp.argsort(-ranking, axis=1).astype(jnp.int32)
    request_order = jnp.arange(requests)
    rank_pick = jnp.where(request_order < CAP, 0, 1 + (request_order - CAP) % (N_SEQ - 1))
    owners = jnp.take_along_axis(ranked, jnp.broadcast_to(rank_pick[None, :], (readers, requests)), axis=1)
    slots = jax.random.randint(jax.random.fold_in(key, 14), (readers, requests), 0, DB_DEV)
    chosen = inverse[owners * DB_DEV + slots]
    mixing = jax.random.randint(jax.random.fold_in(key, 15), (readers, requests), 0, requests * requests) * requests + request_order[None, :]
    shuffle = jnp.argsort(mixing, axis=1)
    chosen = jnp.take_along_axis(chosen, shuffle, axis=1)
    return (block_home, chosen.reshape(SPANS, K).astype(jnp.int32))


def draw_block_home(key, part):
    return plan_blocks(key)[0]


def draw_neighbours(key, part):
    return plan_blocks(key)[1]


def draw_hidden(key, part):
    values = jax.random.normal(jax.random.fold_in(key, 41), (TOKENS, D), jnp.float32)
    return jnp.clip(values, -6.0, 6.0).astype(jnp.bfloat16)


def draw_database(key, part):
    values = jax.random.normal(jax.random.fold_in(key, 51), (N_DP, DB_BLOCKS, BLOCK, E), jnp.float32)
    return jnp.clip(values, -8.0, 8.0).astype(jnp.bfloat16)


def draw_encoder_projection(key, part):
    values = jnp.clip(jax.random.normal(jax.random.fold_in(key, 61), (E, 3 * E), jnp.float32), -6.0, 6.0) * E ** (-0.5)
    return jnp.clip(values, -2.0, 2.0).astype(jnp.bfloat16)


def draw_cross_query(key, part):
    values = jnp.clip(jax.random.normal(jax.random.fold_in(key, 71), (D, D), jnp.float32), -6.0, 6.0) * D ** (-0.5)
    return jnp.clip(values, -2.0, 2.0).astype(jnp.bfloat16)


def draw_cross_keyvalue(key, part):
    values = jnp.clip(jax.random.normal(jax.random.fold_in(key, 81), (2 * D, E), jnp.float32), -6.0, 6.0) * E ** (-0.5)
    return jnp.clip(values, -2.0, 2.0).astype(jnp.bfloat16)


def plant(entries, own_key, smallest, high):
    shape = entries.shape
    index_at = [jax.random.randint(jax.random.fold_in(own_key, axis), (), 0, shape[axis]) for axis in range(len(shape))]
    entries = entries.at[tuple(index_at)].set(smallest)
    longest = shape.index(max(shape))
    index_at[longest] = (index_at[longest] + 1) % shape[longest]
    return entries.at[tuple(index_at)].set(high)


def block_scale(stream_key, shape, cuts, least, top_value):
    level = 1.0
    for dim, parts in cuts:
        draws = jax.random.uniform(jax.random.fold_in(jax.random.fold_in(stream_key, 6), dim), (parts,), jnp.float32, least / len(cuts), top_value / len(cuts))
        level = level * jnp.repeat(jnp.exp(draws), shape[dim] // parts).reshape((-1,) + (1,) * (len(shape) - 1 - dim))
    return level


def gaussian(key, extent, scale, bound, pieces=(), kind=jnp.bfloat16):
    entries = jax.random.normal(key, extent, jnp.float32) * scale
    if len(pieces) > 0:
        entries = block_scale(key, extent, pieces, -0.22, 0.18) * entries
    return jnp.clip(entries, min=-bound, max=bound).astype(kind)


def setup_inputs(seed: int = 0) -> dict:
    seeds = jax.random.split(jax.random.key(seed), 14)
    return {
        "hidden": draw_hidden(jax.random.fold_in(seeds[13], 71), 0),
        "database": draw_database(jax.random.fold_in(seeds[13], 71), 0),
        "block_home": draw_block_home(jax.random.fold_in(seeds[13], 71), 0),
        "neighbours": draw_neighbours(jax.random.fold_in(seeds[13], 71), 0),
        "neighbour_counts": plant(jax.random.randint(seeds[4], (SPANS,), 1, K + 1), jax.random.fold_in(seeds[4], 1), 1, K).astype(jnp.int32),
        "encoder_gain": jnp.clip(1.0 + 0.15 * jax.random.normal(seeds[5], (E,), jnp.float32), 0.25, 1.75),
        "encoder_projection": draw_encoder_projection(jax.random.fold_in(seeds[13], 71), 0),
        "encoder_output": gaussian(seeds[7], (E, E), E ** -0.5, 0.1875),
        "cross_gain": jnp.clip(1.0 + 0.15 * jax.random.normal(seeds[8], (D,), jnp.float32), 0.25, 1.75),
        "cross_query": draw_cross_query(jax.random.fold_in(seeds[13], 71), 0),
        "cross_keyvalue": draw_cross_keyvalue(jax.random.fold_in(seeds[13], 71), 0),
        "cross_output": gaussian(seeds[11], (D, D), D ** -0.5, 0.15625),
        "cotangent": gaussian(seeds[12], (TOKENS, D), 1.0, 6.0, ((0, 32),)),
    }


EPSILON = 1e-06

def rounded(values):
    return lax.optimization_barrier(values.astype(jnp.bfloat16)).astype(jnp.float32)

def rms_norm(values, norm_gain):
    widened = values.astype(jnp.float32)
    return widened * lax.rsqrt(lax.optimization_barrier(jnp.mean(widened * widened, axis=-1, keepdims=True)) + EPSILON) * norm_gain

def encode(blocks, encoder_gain, encoder_projection, encoder_output):
    count, length, width = blocks.shape
    head_count = width // HEAD
    normed = rms_norm(blocks, encoder_gain).astype(jnp.bfloat16)
    projected = jnp.dot(normed.reshape(count * length, width), encoder_projection, preferred_element_type=jnp.float32)
    projected = rounded(projected).reshape(count, length, 3, head_count, HEAD)
    scores = jnp.einsum('bqhd,bkhd->bhqk', projected[:, :, 0], projected[:, :, 1]) * HEAD ** (-0.5)
    weights = rounded(jax.nn.softmax(scores, axis=-1))
    attended = jnp.einsum('bhqk,bkhd->bqhd', weights, projected[:, :, 2]).astype(jnp.bfloat16)
    mixed = jnp.dot(attended.reshape(count * length, width), encoder_output, preferred_element_type=jnp.float32)
    return (blocks.astype(jnp.float32) + mixed.reshape(count, length, width)).astype(jnp.bfloat16)

def attend(queries, keyvalue, key_mask, row_flag, grad_attended):
    groups, rows, width = queries.shape
    key_total = keyvalue.shape[1]
    head_count = width // HEAD
    score_scale = HEAD ** (-0.5)
    query_heads = queries.astype(jnp.float32).reshape(groups, rows, head_count, HEAD)
    key_heads = keyvalue[:, :, :width].astype(jnp.float32).reshape(groups, key_total, head_count, HEAD)
    value_heads = keyvalue[:, :, width:].astype(jnp.float32).reshape(groups, key_total, head_count, HEAD)
    grad_heads = grad_attended.astype(jnp.float32).reshape(groups, rows, head_count, HEAD)
    scores = jnp.einsum('gqhd,gkhd->ghqk', query_heads, key_heads) * score_scale
    scores = jnp.where(key_mask[:, None, None, :], scores, -1e+30)
    chances = jax.nn.softmax(scores, axis=-1) * row_flag[:, None, :, None]
    chances_low = rounded(chances)
    attended = jnp.einsum('ghqk,gkhd->gqhd', chances_low, value_heads).astype(jnp.bfloat16)
    grad_chances = jnp.einsum('gqhd,gkhd->ghqk', grad_heads, value_heads)
    grad_scores = rounded(chances * (grad_chances - lax.optimization_barrier(jnp.sum(chances * grad_chances, axis=-1, keepdims=True))))
    grad_keys = jnp.einsum('ghqk,gqhd->gkhd', grad_scores, query_heads) * score_scale
    grad_values = jnp.einsum('ghqk,gqhd->gkhd', chances_low, grad_heads)
    grad_keyvalue = jnp.concatenate([grad_keys.reshape(groups, key_total, width), grad_values.reshape(groups, key_total, width)], axis=-1).astype(jnp.bfloat16)
    return (attended.reshape(groups, rows, width), grad_keyvalue)

def reference(hidden, database, block_home, neighbours, neighbour_counts, encoder_gain, encoder_projection, encoder_output, cross_gain, cross_query, cross_keyvalue, cross_output, cotangent):
    seq_length = TOK_DEV * N_SEQ
    span_total = seq_length // SPAN
    width = hidden.shape[1]
    feature = database.shape[3]
    normed = rms_norm(hidden, cross_gain).astype(jnp.bfloat16)
    queries = jnp.dot(normed, cross_query, preferred_element_type=jnp.float32).astype(jnp.bfloat16)
    grad_attended = lax.dot_general(cotangent, cross_output, (((1,), (1,)), ((), ())), preferred_element_type=jnp.float32).astype(jnp.bfloat16)

    def shifted(values):
        rows = values.reshape(N_DP, seq_length, width)
        moved = jnp.concatenate([rows[:, SPAN - 1:], jnp.zeros((N_DP, SPAN - 1, width), values.dtype)], axis=1)
        return moved.reshape(N_DP * span_total, SPAN, width)
    query_spans = shifted(queries)
    grad_spans = shifted(grad_attended)
    positions = block_home[neighbours].reshape(N_DP * span_total, K).astype(jnp.int32)
    row_index = (jnp.arange(N_DP * span_total) // span_total).astype(jnp.int32)

    def step(total, inputs):
        row, position, count, query_block, grad_block = inputs
        blocks = database[row][position]
        encoded = encode(blocks, encoder_gain, encoder_projection, encoder_output)
        key_rows = encoded.reshape(K * BLOCK, feature)
        keyvalue = lax.dot_general(key_rows, cross_keyvalue, (((1,), (1,)), ((), ())), preferred_element_type=jnp.float32).astype(jnp.bfloat16)
        key_mask = jnp.arange(K * BLOCK) // BLOCK < count
        attended, grad_keyvalue = attend(query_block[None], keyvalue[None], key_mask[None], jnp.ones((1, SPAN), jnp.float32), grad_block[None])
        term = lax.dot_general(grad_keyvalue[0], key_rows, (((0,), (0,)), ((), ())), preferred_element_type=jnp.float32)
        return (total + term, attended[0])
    start = jnp.zeros((2 * width, feature), jnp.float32)
    keyvalue_grad, attended_spans = lax.scan(step, start, (row_index, positions, neighbour_counts, query_spans, grad_spans))
    attended = attended_spans.reshape(N_DP, seq_length, width)
    attended = jnp.concatenate([jnp.zeros((N_DP, SPAN - 1, width), jnp.bfloat16), attended[:, :seq_length - SPAN + 1]], axis=1).reshape(-1, width)
    cross = jnp.dot(attended, cross_output, preferred_element_type=jnp.float32)
    output = (hidden.astype(jnp.float32) + cross).astype(jnp.bfloat16)
    return (output, keyvalue_grad)
```

```python
import functools

import jax
import jax.numpy as jnp
from jax import lax
from jax.experimental import pallas as pl
from jax.experimental.pallas import tpu as pltpu
from jax.sharding import PartitionSpec as P

HEAD = 128
K = 2
SPAN = 64


EPSILON = 1e-06
MESH = pl.DeviceIdType.MESH


def shifted(block, axis, distance):
    devices = range(lax.axis_size(axis))
    route = [(i - distance, i) for i in devices if i - distance in devices]
    return lax.ppermute(block, axis, route)


def rms_norm(values, norm_gain):
    widened = values.astype(jnp.float32)
    return (
        widened
        * lax.rsqrt(jnp.mean(widened * widened, axis=-1, keepdims=True) + EPSILON)
        * norm_gain
    )


def locate(block_ids, block_home):
    hits = block_ids[..., None] == jnp.arange(block_home.shape[0], dtype=jnp.int32)
    return jnp.sum(jnp.where(hits, block_home, 0), axis=-1)


def request_kernel(n, tile_ref, out_ref, send_sem, recv_sem):
    me = lax.axis_index("seq")
    barrier = pltpu.get_barrier_semaphore()
    for d in range(1, n):
        pl.semaphore_signal(
            barrier, inc=1, device_id={"seq": lax.rem(me + d, n)}, device_id_type=MESH
        )
    pl.semaphore_wait(barrier, n - 1)
    copies = []
    for d in range(1, n):
        copy = pltpu.make_async_remote_copy(
            src_ref=tile_ref,
            dst_ref=out_ref.at[me],
            send_sem=send_sem.at[d],
            recv_sem=recv_sem.at[d],
            device_id={"seq": lax.rem(me + d, n)},
            device_id_type=MESH,
        )
        copy.start()
        copies.append(copy)
    out_ref[me] = tile_ref[...]
    for copy in copies:
        copy.wait()


def exchange_requests(tile, n):
    return pl.pallas_call(
        functools.partial(request_kernel, n),
        out_shape=jax.ShapeDtypeStruct((n,) + tile.shape, tile.dtype),
        in_specs=[pl.BlockSpec(memory_space=pltpu.VMEM)],
        out_specs=pl.BlockSpec(memory_space=pltpu.VMEM),
        scratch_shapes=[pltpu.SemaphoreType.DMA((n,)), pltpu.SemaphoreType.DMA((n,))],
        compiler_params=pltpu.CompilerParams(collective_id=0, has_side_effects=True),
        name="requests",
    )(tile)


def dot(a, b, dims):
    return lax.dot_general(a, b, (dims, ((), ())), preferred_element_type=jnp.float32)


NN = ((1,), (0,))
NT = ((1,), (1,))
TN = ((0,), (0,))


def softmax(scores):
    raised = jnp.exp(scores - jnp.max(scores, axis=-1, keepdims=True))
    return raised / jnp.sum(raised, axis=-1, keepdims=True)


def span_kernel(
    index_ref,
    count_ref,
    first_ref,
    second_ref,
    query_ref,
    grad_ref,
    gain_ref,
    projection_ref,
    encoder_output_ref,
    keyvalue_weight_ref,
    encoded_ref,
    attended_ref,
    grad_keyvalue_ref,
    blocks_ref,
    projected_ref,
    mixed_ref,
    keyvalue_ref,
):
    length, feature = first_ref.shape[1:]
    width = query_ref.shape[1]
    scale = HEAD ** (-0.5)
    blocks_ref[:length] = first_ref[0]
    blocks_ref[length:] = second_ref[0]
    normed = rms_norm(blocks_ref[...], gain_ref[...]).astype(jnp.bfloat16)
    for part in range(3):
        cols = slice(part * feature, (part + 1) * feature)
        projected_ref[:, cols] = dot(normed, projection_ref[:, cols], NN).astype(jnp.bfloat16)
    for b in range(K):
        rows = slice(b * length, (b + 1) * length)
        for h in range(feature // HEAD):
            q = projected_ref[rows, h * HEAD : (h + 1) * HEAD]
            k = projected_ref[rows, feature + h * HEAD : feature + (h + 1) * HEAD]
            v = projected_ref[rows, 2 * feature + h * HEAD : 2 * feature + (h + 1) * HEAD]
            weights = softmax(dot(q, k, NT) * scale).astype(jnp.bfloat16)
            mixed_ref[rows, h * HEAD : (h + 1) * HEAD] = dot(weights, v, NN).astype(jnp.bfloat16)
    mixed = dot(mixed_ref[...], encoder_output_ref[...], NN)
    encoded = (blocks_ref[...].astype(jnp.float32) + mixed).astype(jnp.bfloat16)
    encoded_ref[...] = encoded
    for part in range(2):
        rows = slice(part * width, (part + 1) * width)
        keyvalue_ref[:, rows] = dot(encoded, keyvalue_weight_ref[rows, :], NT).astype(jnp.bfloat16)
    limit = count_ref[pl.program_id(0)] * length
    valid = lax.broadcasted_iota(jnp.int32, (SPAN, K * length), 1) < limit
    for h in range(width // HEAD):
        cols = slice(h * HEAD, (h + 1) * HEAD)
        value_cols = slice(width + h * HEAD, width + (h + 1) * HEAD)
        q = query_ref[:, cols]
        g = grad_ref[:, cols]
        k = keyvalue_ref[:, cols]
        v = keyvalue_ref[:, value_cols]
        chances = softmax(jnp.where(valid, dot(q, k, NT) * scale, -1e30))
        chances_low = chances.astype(jnp.bfloat16)
        attended_ref[:, cols] = dot(chances_low, v, NN).astype(jnp.bfloat16)
        grad_chances = dot(g, v, NT)
        centre = jnp.sum(chances * grad_chances, axis=-1, keepdims=True)
        grad_scores = (chances * (grad_chances - centre)).astype(jnp.bfloat16)
        grad_keyvalue_ref[:, cols] = (dot(grad_scores, q, TN) * scale).astype(jnp.bfloat16)
        grad_keyvalue_ref[:, value_cols] = dot(chances_low, g, TN).astype(jnp.bfloat16)


def span_attention(
    incoming, index, counts, query_rows, grad_rows, gain, projection, encoder_output, cross_keyvalue
):
    _, length, feature = incoming.shape
    tokens, width = query_rows.shape
    spans = tokens // SPAN
    whole = lambda a: pl.BlockSpec(
        a.shape, lambda i, index, count: (0, 0), pipeline_mode=pl.Buffered(1)
    )
    row = lambda r, c: pl.BlockSpec((r, c), lambda i, index, count: (i, 0))
    keys = K * length
    return pl.pallas_call(
        span_kernel,
        grid_spec=pltpu.PrefetchScalarGridSpec(
            num_scalar_prefetch=2,
            grid=(spans,),
            in_specs=[
                pl.BlockSpec((1, length, feature), lambda i, index, count: (index[2 * i], 0, 0)),
                pl.BlockSpec(
                    (1, length, feature), lambda i, index, count: (index[2 * i + 1], 0, 0)
                ),
                row(SPAN, width),
                row(SPAN, width),
                whole(gain),
                whole(projection),
                whole(encoder_output),
                whole(cross_keyvalue),
            ],
            out_specs=[row(keys, feature), row(SPAN, width), row(keys, 2 * width)],
            scratch_shapes=[
                pltpu.VMEM((keys, feature), jnp.bfloat16),
                pltpu.VMEM((keys, 3 * feature), jnp.bfloat16),
                pltpu.VMEM((keys, feature), jnp.bfloat16),
                pltpu.VMEM((keys, 2 * width), jnp.bfloat16),
            ],
        ),
        out_shape=[
            jax.ShapeDtypeStruct((spans * keys, feature), jnp.bfloat16),
            jax.ShapeDtypeStruct((tokens, width), jnp.bfloat16),
            jax.ShapeDtypeStruct((spans * keys, 2 * width), jnp.bfloat16),
        ],
        name="spans",
    )(
        index,
        counts,
        incoming,
        incoming,
        query_rows,
        grad_rows,
        gain,
        projection,
        encoder_output,
        cross_keyvalue,
    )


def bits_of(axis):
    return lax.axis_size(axis).bit_length() - 1


def swap(values, axis, bit):
    return lax.ppermute(
        values, axis, [(i, i ^ (1 << bit)) for i in range(lax.axis_size(axis))]
    )


def reduce_stream(partial, order):
    seq_bits, dp_bits = (bits_of("seq"), bits_of("dp"))
    names = [("seq", b) for b in reversed(range(seq_bits))]
    names += [("dp", b) for b in reversed(range(dp_bits))]
    rows, cols = partial.shape
    values = partial.reshape((2,) * len(names) + (rows >> len(names), cols))
    for stage in order:
        dim = names.index(stage)
        mine = (lax.axis_index(stage[0]) >> stage[1]) & 1
        sent = lax.dynamic_index_in_dim(values, 1 - mine, dim, keepdims=False)
        kept = lax.dynamic_index_in_dim(values, mine, dim, keepdims=False)
        other = swap(sent, *stage)
        values = (kept.astype(jnp.float32) + other.astype(jnp.float32)).astype(jnp.bfloat16)
        names.pop(dim)
    for b in reversed(range(dp_bits)):
        mine = (lax.axis_index("dp") >> b) & 1
        other = swap(values, "dp", b)
        low = jnp.where(mine == 0, values, other)
        high = jnp.where(mine == 0, other, values)
        values = jnp.stack([low, high], axis=dp_bits - 1 - b)
    return values.reshape(-1, cols).astype(jnp.float32)


def stage_orders():
    seq = [("seq", b) for b in range(bits_of("seq"))]
    dp = [("dp", b) for b in range(bits_of("dp"))]
    far = list(reversed(seq[1:]))
    return [dp + seq[:1] + far, dp[:1] + seq[:1] + dp[1:] + far]


def local(
    hidden,
    database,
    block_home,
    neighbours,
    neighbour_counts,
    encoder_gain,
    encoder_projection,
    encoder_output,
    cross_gain,
    cross_query,
    cross_keyvalue,
    cross_output,
    cotangent,
):
    token_count, width = hidden.shape
    shard_blocks, block_length, feature = (database.shape[1], database.shape[2], database.shape[3])
    span_count = token_count // SPAN
    requests = span_count * K
    seq_devices = lax.axis_size("seq")
    reader_index = lax.axis_index("seq")
    capacity = max(2, -(-requests // seq_devices))
    where = locate(neighbours.reshape(-1), block_home)
    owner = where // shard_blocks
    slot = where % shard_blocks
    order = jnp.arange(requests)
    first = ~jnp.any(
        (where[:, None] == where[None, :]) & (order[:, None] > order[None, :]), axis=1
    )
    lower = first[None, :] & (owner[:, None] == owner[None, :]) & (where[None, :] < where[:, None])
    fetch_index = owner * capacity + jnp.sum(lower.astype(jnp.int32), axis=1)
    lanes = -(-seq_devices * capacity // 128) * 128
    chosen = first[:, None] & (fetch_index[:, None] == jnp.arange(lanes, dtype=jnp.int32)[None, :])
    table = jnp.sum(jnp.where(chosen, slot[:, None], 0), axis=0)
    tables = exchange_requests(jnp.broadcast_to(table[None, :], (8, lanes)), seq_devices)
    local_index = lax.dynamic_slice_in_dim(tables[:, 0], reader_index * capacity, capacity, axis=1)
    outgoing = jnp.take(database[0], local_index.reshape(-1), axis=0, mode="clip").reshape(
        seq_devices, capacity, block_length, feature
    )
    incoming = lax.all_to_all(outgoing, "seq", split_axis=0, concat_axis=0, tiled=True)
    normed = rms_norm(hidden, cross_gain).astype(jnp.bfloat16)
    queries = jnp.dot(normed, cross_query, preferred_element_type=jnp.float32).astype(jnp.bfloat16)
    grad_attended = lax.dot_general(
        cotangent, cross_output, (((1,), (1,)), ((), ())), preferred_element_type=jnp.float32
    ).astype(jnp.bfloat16)
    late_queries, late_grads = shifted((queries[: SPAN - 1], grad_attended[: SPAN - 1]), "seq", -1)
    query_rows = jnp.concatenate([queries[SPAN - 1 :], late_queries], axis=0)
    grad_rows = jnp.concatenate([grad_attended[SPAN - 1 :], late_grads], axis=0)
    encoded, attended_rows, grad_keyvalue = span_attention(
        incoming.reshape(seq_devices * capacity, block_length, feature),
        fetch_index,
        neighbour_counts,
        query_rows,
        grad_rows,
        encoder_gain.reshape(1, feature),
        encoder_projection,
        encoder_output,
        cross_keyvalue,
    )
    half = -(-feature // 256) * 128
    streams = []
    for cols, stages in zip((slice(0, half), slice(half, feature)), stage_orders()):
        partial = lax.dot_general(
            grad_keyvalue,
            encoded[:, cols],
            (((0,), (0,)), ((), ())),
            preferred_element_type=jnp.float32,
        ).astype(jnp.bfloat16)
        streams.append(reduce_stream(partial, stages))
    keyvalue_grad = jnp.concatenate(streams, axis=1)
    returned = shifted(attended_rows[token_count - SPAN + 1 :], "seq", 1)
    attended = jnp.concatenate([returned, attended_rows[: token_count - SPAN + 1]], axis=0)
    cross = jnp.dot(attended, cross_output, preferred_element_type=jnp.float32)
    output = (hidden.astype(jnp.float32) + cross).astype(jnp.bfloat16)
    return (output, keyvalue_grad)


def solution(mesh):
    placed = (
        P(("dp", "seq"), None),
        P("dp", "seq", None, None),
        P(),
        P(("dp", "seq"), None),
        P(("dp", "seq")),
        P(),
        P(),
        P(),
        P(),
        P(),
        P(),
        P(),
        P(("dp", "seq"), None),
    )
    return jax.shard_map(
        local,
        mesh=mesh,
        in_specs=placed,
        out_specs=(P(("dp", "seq"), None), P("seq", None)),
        check_vma=False,
    )
```

```python
import functools

import jax
import jax.numpy as jnp
from jax import lax
from jax.experimental import pallas as pl
from jax.experimental.pallas import tpu as pltpu
from jax.sharding import PartitionSpec as P

HEAD = 128
K = 2
SPAN = 64


EPSILON = 1e-06
MESH = pl.DeviceIdType.MESH


def shifted(block, axis, distance):
    devices = range(lax.axis_size(axis))
    route = [(i - distance, i) for i in devices if i - distance in devices]
    return lax.ppermute(block, axis, route)


def rms_norm(values, norm_gain):
    widened = values.astype(jnp.float32)
    return (
        widened
        * lax.rsqrt(jnp.mean(widened * widened, axis=-1, keepdims=True) + EPSILON)
        * norm_gain
    )


def locate(block_ids, block_home):
    hits = block_ids[..., None] == jnp.arange(block_home.shape[0], dtype=jnp.int32)
    return jnp.sum(jnp.where(hits, block_home, 0), axis=-1)


def request_kernel(n, tile_ref, out_ref, send_sem, recv_sem):
    me = lax.axis_index("seq")
    barrier = pltpu.get_barrier_semaphore()
    for d in range(1, n):
        pl.semaphore_signal(
            barrier, inc=1, device_id={"seq": lax.rem(me + d, n)}, device_id_type=MESH
        )
    pl.semaphore_wait(barrier, n - 1)
    copies = []
    for d in range(1, n):
        copy = pltpu.make_async_remote_copy(
            src_ref=tile_ref,
            dst_ref=out_ref.at[me],
            send_sem=send_sem.at[d],
            recv_sem=recv_sem.at[d],
            device_id={"seq": lax.rem(me + d, n)},
            device_id_type=MESH,
        )
        copy.start()
        copies.append(copy)
    out_ref[me] = tile_ref[...]
    for copy in copies:
        copy.wait()


def exchange_requests(tile, n):
    return pl.pallas_call(
        functools.partial(request_kernel, n),
        out_shape=jax.ShapeDtypeStruct((n,) + tile.shape, tile.dtype),
        in_specs=[pl.BlockSpec(memory_space=pltpu.VMEM)],
        out_specs=pl.BlockSpec(memory_space=pltpu.VMEM),
        scratch_shapes=[pltpu.SemaphoreType.DMA((n,)), pltpu.SemaphoreType.DMA((n,))],
        compiler_params=pltpu.CompilerParams(collective_id=0, has_side_effects=True),
        name="requests",
    )(tile)


def dot(a, b, dims):
    return lax.dot_general(a, b, (dims, ((), ())), preferred_element_type=jnp.float32)


NN = ((1,), (0,))
NT = ((1,), (1,))
TN = ((0,), (0,))


def softmax(scores):
    raised = jnp.exp(scores - jnp.max(scores, axis=-1, keepdims=True))
    return raised / jnp.sum(raised, axis=-1, keepdims=True)


def span_kernel(
    index_ref,
    count_ref,
    first_ref,
    second_ref,
    query_ref,
    grad_ref,
    gain_ref,
    projection_ref,
    encoder_output_ref,
    keyvalue_weight_ref,
    encoded_ref,
    attended_ref,
    grad_keyvalue_ref,
    blocks_ref,
    projected_ref,
    mixed_ref,
    keyvalue_ref,
):
    length, feature = first_ref.shape[1:]
    width = query_ref.shape[1]
    scale = HEAD ** (-0.5)
    blocks_ref[:length] = first_ref[0]
    blocks_ref[length:] = second_ref[0]
    normed = rms_norm(blocks_ref[...], gain_ref[...]).astype(jnp.bfloat16)
    for part in range(3):
        cols = slice(part * feature, (part + 1) * feature)
        projected_ref[:, cols] = dot(normed, projection_ref[:, cols], NN).astype(jnp.bfloat16)
    heads = [
        (slice(b * length, (b + 1) * length), h * HEAD)
        for b in range(K)
        for h in range(feature // HEAD)
    ]
    scores = [
        dot(
            projected_ref[rows, at : at + HEAD],
            projected_ref[rows, feature + at : feature + at + HEAD],
            NT,
        )
        * scale
        for rows, at in heads
    ]
    weights = [softmax(score).astype(jnp.bfloat16) for score in scores]
    for (rows, at), weight in zip(heads, weights):
        values = projected_ref[rows, 2 * feature + at : 2 * feature + at + HEAD]
        mixed_ref[rows, at : at + HEAD] = dot(weight, values, NN).astype(jnp.bfloat16)
    mixed = dot(mixed_ref[...], encoder_output_ref[...], NN)
    encoded = (blocks_ref[...].astype(jnp.float32) + mixed).astype(jnp.bfloat16)
    encoded_ref[...] = encoded
    for part in range(2):
        rows = slice(part * width, (part + 1) * width)
        keyvalue_ref[:, rows] = dot(encoded, keyvalue_weight_ref[rows, :], NT).astype(jnp.bfloat16)
    limit = count_ref[pl.program_id(0)] * length
    valid = lax.broadcasted_iota(jnp.int32, (SPAN, K * length), 1) < limit
    heads = [
        (slice(h * HEAD, (h + 1) * HEAD), slice(width + h * HEAD, width + (h + 1) * HEAD))
        for h in range(width // HEAD)
    ]
    scores = [dot(query_ref[:, c], keyvalue_ref[:, c], NT) * scale for c, _ in heads]
    grad_chances = [dot(grad_ref[:, c], keyvalue_ref[:, v], NT) for c, v in heads]
    chances = [softmax(jnp.where(valid, score, -1e30)) for score in scores]
    chances_low = [chance.astype(jnp.bfloat16) for chance in chances]
    grad_scores = [
        (chance * (grad - jnp.sum(chance * grad, axis=-1, keepdims=True))).astype(jnp.bfloat16)
        for chance, grad in zip(chances, grad_chances)
    ]
    for (c, v), low, grad in zip(heads, chances_low, grad_scores):
        attended_ref[:, c] = dot(low, keyvalue_ref[:, v], NN).astype(jnp.bfloat16)
        grad_keyvalue_ref[:, c] = (dot(grad, query_ref[:, c], TN) * scale).astype(jnp.bfloat16)
        grad_keyvalue_ref[:, v] = dot(low, grad_ref[:, c], TN).astype(jnp.bfloat16)


def span_attention(
    incoming, index, counts, query_rows, grad_rows, gain, projection, encoder_output, cross_keyvalue
):
    _, length, feature = incoming.shape
    tokens, width = query_rows.shape
    spans = tokens // SPAN
    whole = lambda a: pl.BlockSpec(
        a.shape, lambda i, index, count: (0, 0), pipeline_mode=pl.Buffered(1)
    )
    row = lambda r, c: pl.BlockSpec((r, c), lambda i, index, count: (i, 0))
    keys = K * length
    return pl.pallas_call(
        span_kernel,
        grid_spec=pltpu.PrefetchScalarGridSpec(
            num_scalar_prefetch=2,
            grid=(spans,),
            in_specs=[
                pl.BlockSpec((1, length, feature), lambda i, index, count: (index[2 * i], 0, 0)),
                pl.BlockSpec(
                    (1, length, feature), lambda i, index, count: (index[2 * i + 1], 0, 0)
                ),
                row(SPAN, width),
                row(SPAN, width),
                whole(gain),
                whole(projection),
                whole(encoder_output),
                whole(cross_keyvalue),
            ],
            out_specs=[row(keys, feature), row(SPAN, width), row(keys, 2 * width)],
            scratch_shapes=[
                pltpu.VMEM((keys, feature), jnp.bfloat16),
                pltpu.VMEM((keys, 3 * feature), jnp.bfloat16),
                pltpu.VMEM((keys, feature), jnp.bfloat16),
                pltpu.VMEM((keys, 2 * width), jnp.bfloat16),
            ],
        ),
        out_shape=[
            jax.ShapeDtypeStruct((spans * keys, feature), jnp.bfloat16),
            jax.ShapeDtypeStruct((tokens, width), jnp.bfloat16),
            jax.ShapeDtypeStruct((spans * keys, 2 * width), jnp.bfloat16),
        ],
        name="spans",
    )(
        index,
        counts,
        incoming,
        incoming,
        query_rows,
        grad_rows,
        gain,
        projection,
        encoder_output,
        cross_keyvalue,
    )


def bits_of(axis):
    return lax.axis_size(axis).bit_length() - 1


def reduce_kernel(
    streams,
    partial_ref,
    attended_ref,
    weight_ref,
    hidden_ref,
    sum_ref,
    output_ref,
    *scratch,
):
    stage_count = len(streams[0][1])
    buffers = [
        scratch[s * stage_count : (s + 1) * stage_count] for s in range(len(streams))
    ]
    send_sem, recv_sem, gather_send, gather_recv = scratch[len(streams) * stage_count :]
    dp, dp_size = lax.axis_index("dp"), lax.axis_size("dp")
    names = [("seq", b) for b in reversed(range(bits_of("seq")))]
    names += [("dp", b) for b in reversed(range(bits_of("dp")))]
    mine = {name: (lax.axis_index(name[0]) // (1 << name[1])) % 2 for name in names}

    def partner(name):
        return {name[0]: lax.axis_index(name[0]) + (1 - 2 * mine[name]) * (1 << name[1])}

    dp_others = [{"dp": lax.rem(dp + d, dp_size)} for d in range(1, dp_size)]
    barrier = pltpu.get_barrier_semaphore()
    greeted = dp_others + [partner(name) for name in names if name[0] == "seq"]
    for device in greeted:
        pl.semaphore_signal(barrier, inc=1, device_id=device, device_id_type=MESH)
    pl.semaphore_wait(barrier, len(greeted))

    def source(s, k):
        if k > 0:
            return buffers[s][k - 1], slice(None)
        return partial_ref, streams[s][0]

    def runs(s, k):
        left = [name for name in names if name not in streams[s][1][:k]]
        name = streams[s][1][k]
        place = len(left) - 1 - left.index(name)
        run = 1 << place
        return name, run, (1 << (len(left) - 1)) // run

    def start(s, k):
        name, run, count = runs(s, k)
        held, cols = source(s, k)
        for j in range(count):
            pltpu.make_async_remote_copy(
                src_ref=held.at[pl.ds(2 * j * run + (1 - mine[name]) * run, run), :, cols],
                dst_ref=buffers[s][k].at[pl.ds(j * run, run)],
                send_sem=send_sem.at[s, k],
                recv_sem=recv_sem.at[s, k],
                device_id=partner(name),
                device_id_type=MESH,
            ).start()

    def whole(s, k):
        return pltpu.make_async_remote_copy(
            src_ref=buffers[s][k],
            dst_ref=buffers[s][k],
            send_sem=send_sem.at[s, k],
            recv_sem=recv_sem.at[s, k],
            device_id=partner(streams[s][1][k]),
            device_id_type=MESH,
        )

    def finish(s, k):
        name, run, count = runs(s, k)
        held, cols = source(s, k)
        whole(s, k).wait_recv()
        for j in range(count):
            kept = held[pl.ds(2 * j * run + mine[name] * run, run), :, cols]
            here = slice(j * run, (j + 1) * run)
            other = buffers[s][k][here]
            buffers[s][k][here] = (
                kept.astype(jnp.float32) + other.astype(jnp.float32)
            ).astype(jnp.bfloat16)

    for s in range(len(streams)):
        start(s, 0)
    gathers = []
    for k in range(stage_count):
        for s in range(len(streams)):
            finish(s, k)
            if k + 1 < stage_count:
                start(s, k + 1)
                continue
            cols = streams[s][0]
            sum_ref[dp, :, cols] = buffers[s][k][0]
            for d, device in enumerate(dp_others):
                copy = pltpu.make_async_remote_copy(
                    src_ref=buffers[s][k].at[0],
                    dst_ref=sum_ref.at[dp, :, cols],
                    send_sem=gather_send.at[s, d],
                    recv_sem=gather_recv.at[s, d],
                    device_id=device,
                    device_id_type=MESH,
                )
                copy.start()
                gathers.append(copy)
        if k == 0:
            cross = dot(attended_ref[...], weight_ref[...], NN)
            output_ref[...] = (hidden_ref[...].astype(jnp.float32) + cross).astype(jnp.bfloat16)
    for s in range(len(streams)):
        for k in range(stage_count):
            whole(s, k).wait_send()
    for copy in gathers:
        copy.wait()


def reduce_gradient(partial, attended, cross_output, hidden):
    rows, feature = partial.shape
    dp_size = lax.axis_size("dp")
    stage_count = bits_of("seq") + bits_of("dp")
    piece = rows >> stage_count
    edges = list(range(0, feature, 256)) + [feature]
    orders = stage_orders()
    streams = [
        (slice(low, high), orders[i % len(orders)])
        for i, (low, high) in enumerate(zip(edges[:-1], edges[1:]))
    ]
    buffers = [
        pltpu.VMEM((1 << (stage_count - 1 - k), piece, cols.stop - cols.start), jnp.bfloat16)
        for cols, _ in streams
        for k in range(stage_count)
    ]
    count = len(streams)
    vmem = pl.BlockSpec(memory_space=pltpu.VMEM)
    total, output = pl.pallas_call(
        functools.partial(reduce_kernel, streams),
        out_shape=[
            jax.ShapeDtypeStruct((dp_size, piece, feature), jnp.bfloat16),
            jax.ShapeDtypeStruct(hidden.shape, jnp.bfloat16),
        ],
        in_specs=[vmem] * 4,
        out_specs=[vmem] * 2,
        scratch_shapes=buffers
        + [
            pltpu.SemaphoreType.DMA((count, stage_count)),
            pltpu.SemaphoreType.DMA((count, stage_count)),
            pltpu.SemaphoreType.DMA((count, dp_size - 1)),
            pltpu.SemaphoreType.DMA((count, dp_size - 1)),
        ],
        compiler_params=pltpu.CompilerParams(collective_id=1, has_side_effects=True),
        name="reduce",
    )(partial.reshape(1 << stage_count, piece, feature), attended, cross_output, hidden)
    return total.reshape(dp_size * piece, feature).astype(jnp.float32), output


def stage_orders():
    seq = [("seq", b) for b in range(bits_of("seq"))]
    dp = [("dp", b) for b in range(bits_of("dp"))]
    far = list(reversed(seq[1:]))
    return [dp + seq[:1] + far, dp[:1] + seq[:1] + dp[1:] + far]


def local(
    hidden,
    database,
    block_home,
    neighbours,
    neighbour_counts,
    encoder_gain,
    encoder_projection,
    encoder_output,
    cross_gain,
    cross_query,
    cross_keyvalue,
    cross_output,
    cotangent,
):
    token_count, width = hidden.shape
    shard_blocks, block_length, feature = (database.shape[1], database.shape[2], database.shape[3])
    span_count = token_count // SPAN
    requests = span_count * K
    seq_devices = lax.axis_size("seq")
    reader_index = lax.axis_index("seq")
    capacity = max(2, -(-requests // seq_devices))
    where = locate(neighbours.reshape(-1), block_home)
    owner = where // shard_blocks
    slot = where % shard_blocks
    order = jnp.arange(requests)
    first = ~jnp.any(
        (where[:, None] == where[None, :]) & (order[:, None] > order[None, :]), axis=1
    )
    lower = first[None, :] & (owner[:, None] == owner[None, :]) & (where[None, :] < where[:, None])
    fetch_index = owner * capacity + jnp.sum(lower.astype(jnp.int32), axis=1)
    lanes = -(-seq_devices * capacity // 128) * 128
    chosen = first[:, None] & (fetch_index[:, None] == jnp.arange(lanes, dtype=jnp.int32)[None, :])
    table = jnp.sum(jnp.where(chosen, slot[:, None], 0), axis=0)
    tables = exchange_requests(jnp.broadcast_to(table[None, :], (8, lanes)), seq_devices)
    local_index = lax.dynamic_slice_in_dim(tables[:, 0], reader_index * capacity, capacity, axis=1)
    outgoing = jnp.take(database[0], local_index.reshape(-1), axis=0, mode="clip").reshape(
        seq_devices, capacity, block_length, feature
    )
    incoming = lax.all_to_all(outgoing, "seq", split_axis=0, concat_axis=0, tiled=True)
    normed = rms_norm(hidden, cross_gain).astype(jnp.bfloat16)
    queries = jnp.dot(normed, cross_query, preferred_element_type=jnp.float32).astype(jnp.bfloat16)
    grad_attended = lax.dot_general(
        cotangent, cross_output, (((1,), (1,)), ((), ())), preferred_element_type=jnp.float32
    ).astype(jnp.bfloat16)
    late_queries, late_grads = shifted((queries[: SPAN - 1], grad_attended[: SPAN - 1]), "seq", -1)
    query_rows = jnp.concatenate([queries[SPAN - 1 :], late_queries], axis=0)
    grad_rows = jnp.concatenate([grad_attended[SPAN - 1 :], late_grads], axis=0)
    encoded, attended_rows, grad_keyvalue = span_attention(
        incoming.reshape(seq_devices * capacity, block_length, feature),
        fetch_index,
        neighbour_counts,
        query_rows,
        grad_rows,
        encoder_gain.reshape(1, feature),
        encoder_projection,
        encoder_output,
        cross_keyvalue,
    )
    partial = lax.dot_general(
        grad_keyvalue, encoded, (((0,), (0,)), ((), ())), preferred_element_type=jnp.float32
    ).astype(jnp.bfloat16)
    returned = shifted(attended_rows[token_count - SPAN + 1 :], "seq", 1)
    attended = jnp.concatenate([returned, attended_rows[: token_count - SPAN + 1]], axis=0)
    keyvalue_grad, output = reduce_gradient(partial, attended, cross_output, hidden)
    return (output, keyvalue_grad)


def solution(mesh):
    placed = (
        P(("dp", "seq"), None),
        P("dp", "seq", None, None),
        P(),
        P(("dp", "seq"), None),
        P(("dp", "seq")),
        P(),
        P(),
        P(),
        P(),
        P(),
        P(),
        P(),
        P(("dp", "seq"), None),
    )
    return jax.shard_map(
        local,
        mesh=mesh,
        in_specs=placed,
        out_specs=(P(("dp", "seq"), None), P("seq", None)),
        check_vma=False,
    )
```

```python
import functools

import jax
import jax.numpy as jnp
from jax import lax
from jax.experimental import pallas as pl
from jax.experimental.pallas import tpu as pltpu
from jax.sharding import PartitionSpec as P

HEAD = 128
K = 2
SPAN = 64


EPSILON = 1e-06
MESH = pl.DeviceIdType.MESH


def shifted(block, axis, distance):
    devices = range(lax.axis_size(axis))
    route = [(i - distance, i) for i in devices if i - distance in devices]
    return lax.ppermute(block, axis, route)


def rms_norm(values, norm_gain):
    widened = values.astype(jnp.float32)
    return (
        widened
        * lax.rsqrt(jnp.mean(widened * widened, axis=-1, keepdims=True) + EPSILON)
        * norm_gain
    )


def locate(block_ids, block_home):
    hits = block_ids[..., None] == jnp.arange(block_home.shape[0], dtype=jnp.int32)
    return jnp.sum(jnp.where(hits, block_home, 0), axis=-1)


def request_kernel(n, tile_ref, out_ref, send_sem, recv_sem):
    me = lax.axis_index("seq")
    barrier = pltpu.get_barrier_semaphore()
    for d in range(1, n):
        pl.semaphore_signal(
            barrier, inc=1, device_id={"seq": lax.rem(me + d, n)}, device_id_type=MESH
        )
    pl.semaphore_wait(barrier, n - 1)
    copies = []
    for d in range(1, n):
        copy = pltpu.make_async_remote_copy(
            src_ref=tile_ref,
            dst_ref=out_ref.at[me],
            send_sem=send_sem.at[d],
            recv_sem=recv_sem.at[d],
            device_id={"seq": lax.rem(me + d, n)},
            device_id_type=MESH,
        )
        copy.start()
        copies.append(copy)
    out_ref[me] = tile_ref[...]
    for copy in copies:
        copy.wait()


def exchange_requests(tile, n):
    return pl.pallas_call(
        functools.partial(request_kernel, n),
        out_shape=jax.ShapeDtypeStruct((n,) + tile.shape, tile.dtype),
        in_specs=[pl.BlockSpec(memory_space=pltpu.VMEM)],
        out_specs=pl.BlockSpec(memory_space=pltpu.VMEM),
        scratch_shapes=[pltpu.SemaphoreType.DMA((n,)), pltpu.SemaphoreType.DMA((n,))],
        compiler_params=pltpu.CompilerParams(collective_id=0, has_side_effects=True),
        name="requests",
    )(tile)


def dot(a, b, dims):
    return lax.dot_general(a, b, (dims, ((), ())), preferred_element_type=jnp.float32)


NN = ((1,), (0,))
NT = ((1,), (1,))
TN = ((0,), (0,))


def softmax(scores):
    raised = jnp.exp(scores - jnp.max(scores, axis=-1, keepdims=True))
    return raised / jnp.sum(raised, axis=-1, keepdims=True)


def span_kernel(
    index_ref,
    count_ref,
    first_ref,
    second_ref,
    query_ref,
    grad_ref,
    gain_ref,
    projection_ref,
    encoder_output_ref,
    keyvalue_weight_ref,
    encoded_ref,
    attended_ref,
    grad_keyvalue_ref,
    blocks_ref,
    projected_ref,
    mixed_ref,
    keyvalue_ref,
):
    length, feature = first_ref.shape[1:]
    width = query_ref.shape[1]
    scale = HEAD ** (-0.5)
    blocks_ref[:length] = first_ref[0]
    blocks_ref[length:] = second_ref[0]
    normed = rms_norm(blocks_ref[...], gain_ref[...]).astype(jnp.bfloat16)
    for part in range(3):
        cols = slice(part * feature, (part + 1) * feature)
        projected_ref[:, cols] = dot(normed, projection_ref[:, cols], NN).astype(jnp.bfloat16)
    heads = [
        (slice(b * length, (b + 1) * length), h * HEAD)
        for b in range(K)
        for h in range(feature // HEAD)
    ]
    scores = [
        dot(
            projected_ref[rows, at : at + HEAD],
            projected_ref[rows, feature + at : feature + at + HEAD],
            NT,
        )
        * scale
        for rows, at in heads
    ]
    weights = [softmax(score).astype(jnp.bfloat16) for score in scores]
    for (rows, at), weight in zip(heads, weights):
        values = projected_ref[rows, 2 * feature + at : 2 * feature + at + HEAD]
        mixed_ref[rows, at : at + HEAD] = dot(weight, values, NN).astype(jnp.bfloat16)
    mixed = dot(mixed_ref[...], encoder_output_ref[...], NN)
    encoded = (blocks_ref[...].astype(jnp.float32) + mixed).astype(jnp.bfloat16)
    encoded_ref[...] = encoded
    for part in range(2):
        rows = slice(part * width, (part + 1) * width)
        keyvalue_ref[:, rows] = dot(encoded, keyvalue_weight_ref[rows, :], NT).astype(jnp.bfloat16)
    limit = count_ref[pl.program_id(0)] * length
    valid = lax.broadcasted_iota(jnp.int32, (SPAN, K * length), 1) < limit
    heads = [
        (slice(h * HEAD, (h + 1) * HEAD), slice(width + h * HEAD, width + (h + 1) * HEAD))
        for h in range(width // HEAD)
    ]
    scores = [dot(query_ref[:, c], keyvalue_ref[:, c], NT) * scale for c, _ in heads]
    grad_chances = [dot(grad_ref[:, c], keyvalue_ref[:, v], NT) for c, v in heads]
    chances = [softmax(jnp.where(valid, score, -1e30)) for score in scores]
    chances_low = [chance.astype(jnp.bfloat16) for chance in chances]
    grad_scores = [
        (chance * (grad - jnp.sum(chance * grad, axis=-1, keepdims=True))).astype(jnp.bfloat16)
        for chance, grad in zip(chances, grad_chances)
    ]
    for (c, v), low, grad in zip(heads, chances_low, grad_scores):
        attended_ref[:, c] = dot(low, keyvalue_ref[:, v], NN).astype(jnp.bfloat16)
        grad_keyvalue_ref[:, c] = (dot(grad, query_ref[:, c], TN) * scale).astype(jnp.bfloat16)
        grad_keyvalue_ref[:, v] = dot(low, grad_ref[:, c], TN).astype(jnp.bfloat16)


def span_attention(
    incoming, index, counts, query_rows, grad_rows, gain, projection, encoder_output, cross_keyvalue
):
    _, length, feature = incoming.shape
    tokens, width = query_rows.shape
    spans = tokens // SPAN
    whole = lambda a: pl.BlockSpec(
        a.shape, lambda i, index, count: (0, 0), pipeline_mode=pl.Buffered(1)
    )
    row = lambda r, c: pl.BlockSpec((r, c), lambda i, index, count: (i, 0))
    keys = K * length
    return pl.pallas_call(
        span_kernel,
        grid_spec=pltpu.PrefetchScalarGridSpec(
            num_scalar_prefetch=2,
            grid=(spans,),
            in_specs=[
                pl.BlockSpec((1, length, feature), lambda i, index, count: (index[2 * i], 0, 0)),
                pl.BlockSpec(
                    (1, length, feature), lambda i, index, count: (index[2 * i + 1], 0, 0)
                ),
                row(SPAN, width),
                row(SPAN, width),
                whole(gain),
                whole(projection),
                whole(encoder_output),
                whole(cross_keyvalue),
            ],
            out_specs=[row(keys, feature), row(SPAN, width), row(keys, 2 * width)],
            scratch_shapes=[
                pltpu.VMEM((keys, feature), jnp.bfloat16),
                pltpu.VMEM((keys, 3 * feature), jnp.bfloat16),
                pltpu.VMEM((keys, feature), jnp.bfloat16),
                pltpu.VMEM((keys, 2 * width), jnp.bfloat16),
            ],
        ),
        out_shape=[
            jax.ShapeDtypeStruct((spans * keys, feature), jnp.bfloat16),
            jax.ShapeDtypeStruct((tokens, width), jnp.bfloat16),
            jax.ShapeDtypeStruct((spans * keys, 2 * width), jnp.bfloat16),
        ],
        name="spans",
    )(
        index,
        counts,
        incoming,
        incoming,
        query_rows,
        grad_rows,
        gain,
        projection,
        encoder_output,
        cross_keyvalue,
    )


def bits_of(axis):
    return lax.axis_size(axis).bit_length() - 1


def reduce_kernel(
    streams,
    partial_ref,
    attended_ref,
    weight_ref,
    hidden_ref,
    sum_ref,
    output_ref,
    *scratch,
):
    stage_count = len(streams[0][1])
    buffers = [
        scratch[s * stage_count : (s + 1) * stage_count] for s in range(len(streams))
    ]
    send_sem, recv_sem, gather_send, gather_recv = scratch[len(streams) * stage_count :]
    dp, dp_size = lax.axis_index("dp"), lax.axis_size("dp")
    names = [("seq", b) for b in reversed(range(bits_of("seq")))]
    names += [("dp", b) for b in reversed(range(bits_of("dp")))]
    mine = {name: (lax.axis_index(name[0]) // (1 << name[1])) % 2 for name in names}

    def partner(name):
        return {name[0]: lax.axis_index(name[0]) + (1 - 2 * mine[name]) * (1 << name[1])}

    dp_others = [{"dp": lax.rem(dp + d, dp_size)} for d in range(1, dp_size)]
    barrier = pltpu.get_barrier_semaphore()
    greeted = dp_others + [partner(name) for name in names if name[0] == "seq"]
    for device in greeted:
        pl.semaphore_signal(barrier, inc=1, device_id=device, device_id_type=MESH)
    pl.semaphore_wait(barrier, len(greeted))

    def source(s, k):
        if k > 0:
            return buffers[s][k - 1], slice(None)
        return partial_ref, streams[s][0]

    def half(s, k, which):
        left = [name for name in names if name not in streams[s][1][:k]]
        name = streams[s][1][k]
        picks = [which if other == name else slice(None) for other in left]
        return tuple(picks)

    def start(s, k):
        name = streams[s][1][k]
        held, rows = source(s, k)
        pltpu.make_async_remote_copy(
            src_ref=held.at[half(s, k, 1 - mine[name]) + (rows,)],
            dst_ref=buffers[s][k],
            send_sem=send_sem.at[s, k],
            recv_sem=recv_sem.at[s, k],
            device_id=partner(name),
            device_id_type=MESH,
        ).start()

    def whole(s, k):
        return pltpu.make_async_remote_copy(
            src_ref=buffers[s][k],
            dst_ref=buffers[s][k],
            send_sem=send_sem.at[s, k],
            recv_sem=recv_sem.at[s, k],
            device_id=partner(streams[s][1][k]),
            device_id_type=MESH,
        )

    def finish(s, k):
        name = streams[s][1][k]
        held, rows = source(s, k)
        whole(s, k).wait_recv()
        kept = held[half(s, k, mine[name]) + (rows,)]
        buffers[s][k][...] = (
            kept.astype(jnp.float32) + buffers[s][k][...].astype(jnp.float32)
        ).astype(jnp.bfloat16)

    for s in range(len(streams)):
        start(s, 0)
    gathers = []
    for k in range(stage_count):
        for s in range(len(streams)):
            finish(s, k)
            if k + 1 < stage_count:
                start(s, k + 1)
                continue
            rows = streams[s][0]
            sum_ref[dp, rows] = buffers[s][k][...]
            for d, device in enumerate(dp_others):
                copy = pltpu.make_async_remote_copy(
                    src_ref=buffers[s][k],
                    dst_ref=sum_ref.at[dp, rows],
                    send_sem=gather_send.at[s, d],
                    recv_sem=gather_recv.at[s, d],
                    device_id=device,
                    device_id_type=MESH,
                )
                copy.start()
                gathers.append(copy)
        if k == 0:
            cross = dot(attended_ref[...], weight_ref[...], NN)
            output_ref[...] = (hidden_ref[...].astype(jnp.float32) + cross).astype(jnp.bfloat16)
    for s in range(len(streams)):
        for k in range(stage_count):
            whole(s, k).wait_send()
    for copy in gathers:
        copy.wait()


def reduce_gradient(partial, attended, cross_output, hidden):
    total_rows, feature = partial.shape
    dp_size = lax.axis_size("dp")
    stage_count = bits_of("seq") + bits_of("dp")
    piece = total_rows >> stage_count
    step = 16 if piece % 16 == 0 else piece
    edges = list(range(0, piece, step)) + [piece]
    orders = stage_orders()
    streams = [
        (slice(low, high), orders[i % len(orders)])
        for i, (low, high) in enumerate(zip(edges[:-1], edges[1:]))
    ]
    buffers = [
        pltpu.VMEM((2,) * (stage_count - 1 - k) + (rows.stop - rows.start, feature), jnp.bfloat16)
        for rows, _ in streams
        for k in range(stage_count)
    ]
    count = len(streams)
    vmem = pl.BlockSpec(memory_space=pltpu.VMEM)
    total, output = pl.pallas_call(
        functools.partial(reduce_kernel, streams),
        out_shape=[
            jax.ShapeDtypeStruct((dp_size, piece, feature), jnp.bfloat16),
            jax.ShapeDtypeStruct(hidden.shape, jnp.bfloat16),
        ],
        in_specs=[vmem] * 4,
        out_specs=[vmem] * 2,
        scratch_shapes=buffers
        + [
            pltpu.SemaphoreType.DMA((count, stage_count)),
            pltpu.SemaphoreType.DMA((count, stage_count)),
            pltpu.SemaphoreType.DMA((count, dp_size - 1)),
            pltpu.SemaphoreType.DMA((count, dp_size - 1)),
        ],
        compiler_params=pltpu.CompilerParams(collective_id=1, has_side_effects=True),
        name="reduce",
    )(partial.reshape((2,) * stage_count + (piece, feature)), attended, cross_output, hidden)
    return total.reshape(dp_size * piece, feature).astype(jnp.float32), output


def stage_orders():
    dp = [("dp", b) for b in range(bits_of("dp"))]
    seq = [("seq", b) for b in range(bits_of("seq"))]
    links = [dp[1:], seq[:1], seq[1:2]]
    turns = [links[i:] + links[:i] for i in range(len(links))]
    return [dp[:1] + sum(turn, []) + seq[2:] for turn in turns]


def local(
    hidden,
    database,
    block_home,
    neighbours,
    neighbour_counts,
    encoder_gain,
    encoder_projection,
    encoder_output,
    cross_gain,
    cross_query,
    cross_keyvalue,
    cross_output,
    cotangent,
):
    token_count, width = hidden.shape
    shard_blocks, block_length, feature = (database.shape[1], database.shape[2], database.shape[3])
    span_count = token_count // SPAN
    requests = span_count * K
    seq_devices = lax.axis_size("seq")
    reader_index = lax.axis_index("seq")
    capacity = max(2, -(-requests // seq_devices))
    where = locate(neighbours.reshape(-1), block_home)
    owner = where // shard_blocks
    slot = where % shard_blocks
    order = jnp.arange(requests)
    first = ~jnp.any(
        (where[:, None] == where[None, :]) & (order[:, None] > order[None, :]), axis=1
    )
    lower = first[None, :] & (owner[:, None] == owner[None, :]) & (where[None, :] < where[:, None])
    fetch_index = owner * capacity + jnp.sum(lower.astype(jnp.int32), axis=1)
    lanes = -(-seq_devices * capacity // 128) * 128
    chosen = first[:, None] & (fetch_index[:, None] == jnp.arange(lanes, dtype=jnp.int32)[None, :])
    table = jnp.sum(jnp.where(chosen, slot[:, None], 0), axis=0)
    tables = exchange_requests(jnp.broadcast_to(table[None, :], (8, lanes)), seq_devices)
    local_index = lax.dynamic_slice_in_dim(tables[:, 0], reader_index * capacity, capacity, axis=1)
    outgoing = jnp.take(database[0], local_index.reshape(-1), axis=0, mode="clip").reshape(
        seq_devices, capacity, block_length, feature
    )
    incoming = lax.all_to_all(outgoing, "seq", split_axis=0, concat_axis=0, tiled=True)
    normed = rms_norm(hidden, cross_gain).astype(jnp.bfloat16)
    queries = jnp.dot(normed, cross_query, preferred_element_type=jnp.float32).astype(jnp.bfloat16)
    grad_attended = lax.dot_general(
        cotangent, cross_output, (((1,), (1,)), ((), ())), preferred_element_type=jnp.float32
    ).astype(jnp.bfloat16)
    late_queries, late_grads = shifted((queries[: SPAN - 1], grad_attended[: SPAN - 1]), "seq", -1)
    query_rows = jnp.concatenate([queries[SPAN - 1 :], late_queries], axis=0)
    grad_rows = jnp.concatenate([grad_attended[SPAN - 1 :], late_grads], axis=0)
    encoded, attended_rows, grad_keyvalue = span_attention(
        incoming.reshape(seq_devices * capacity, block_length, feature),
        fetch_index,
        neighbour_counts,
        query_rows,
        grad_rows,
        encoder_gain.reshape(1, feature),
        encoder_projection,
        encoder_output,
        cross_keyvalue,
    )
    partial = lax.dot_general(
        grad_keyvalue, encoded, (((0,), (0,)), ((), ())), preferred_element_type=jnp.float32
    ).astype(jnp.bfloat16)
    returned = shifted(attended_rows[token_count - SPAN + 1 :], "seq", 1)
    attended = jnp.concatenate([returned, attended_rows[: token_count - SPAN + 1]], axis=0)
    keyvalue_grad, output = reduce_gradient(partial, attended, cross_output, hidden)
    return (output, keyvalue_grad)


def solution(mesh):
    placed = (
        P(("dp", "seq"), None),
        P("dp", "seq", None, None),
        P(),
        P(("dp", "seq"), None),
        P(("dp", "seq")),
        P(),
        P(),
        P(),
        P(),
        P(),
        P(),
        P(),
        P(("dp", "seq"), None),
    )
    return jax.shard_map(
        local,
        mesh=mesh,
        in_specs=placed,
        out_specs=(P(("dp", "seq"), None), P("seq", None)),
        check_vma=False,
    )
```
